32 devices in a mesh: groups: 2 (over y), lat: 4 (over z), depth: 2 (over x), rock: 2 (over core).
Axes of the slice: x: 2, y: 2, z: 4, core: 2. Of those that a mesh axis runs over, the one named last changes fastest.
Arguments:
- incident: float32 [2, 128, 512], P(None, ('groups', 'lat')), parts along dimension 1, may hold values from -6 to 6
- phase: float32 [16, 128, 512], P('depth', ('groups', 'lat'), 'rock'), parts along dimension 1, may hold values from -3.140625 to 3.140625
- deviation: float32 [4], P(('groups', 'rock')), parts along dimension 0, may hold values from -0.4 to 0.4
Outputs:
- slab_exits: float32 [2, 4, 2, 128, 512], P('depth', None, 'rock', ('groups', 'lat')), parts along dimension 3
The draws below stay inside these ranges and needn't reach their ends.
There are 2 independent parts, one for each index of `groups`. The reference program is written for one: setup_inputs(seed, part) draws one part's arguments, and reference() takes and returns one part's arrays. A program takes and returns all parts, laid end to end along the dimension named above; each array names one. Nothing has to cross between parts.
All inputs are finite; a program needn't handle non-finite values.
Results may differ from the reference program's by a relative error of at most 0.00002.
Values sent between devices are 32-bit elements; how exact they have to be, the bound alone decides.
No kernel may reach another device: no remote copies, remote signals or barrier semaphores. Data moves between devices by JAX's collectives and lax.ppermute only.
A program may use at most 64 MiB of HBM per device.

```python
import jax
import jax.numpy as jnp

PLANES = 8
NY = 512
ANGLES = 2
NX = 64
NZ = 16


def block_scale(own_key, extent, pieces, low, largest):
    factor_of, own = 1.0, jax.random.fold_in(own_key, 6)
    for dim, blocks in pieces:
        heights = jnp.exp(jax.random.uniform(jax.random.fold_in(own, dim), (blocks,), jnp.float32, low / len(pieces), largest / len(pieces)))
        factor_of = factor_of * jnp.repeat(heights, extent[dim] // blocks).reshape([-1 if axis == dim else 1 for axis in range(len(extent))])
    return factor_of


def gaussian(key, shape, width, bound, pieces=(), held_as=jnp.bfloat16):
    array = jax.random.normal(key, shape, jnp.float32) * width
    if len(pieces) > 0:
        array = block_scale(key, shape, pieces, -0.22, 0.18) * array
    return jnp.clip(array, min=-bound, max=bound).astype(held_as)


def setup_inputs(seed: int = 0, part: int = 0) -> dict:
    seeds = jax.random.split(jax.random.key(seed), 4)
    own_keys = jax.random.split(jax.random.fold_in(seeds[3], part), 4)
    return {
        "incident": gaussian(own_keys[0], (2, NX, NY), 1.0, 6.0, ((1, 4),), jnp.float32),
        "phase": jnp.clip(jax.random.uniform(own_keys[1], (NZ, NX, NY), jnp.float32, -3.140625, 3.140625), -3.140625, 3.140625),
        "deviation": jnp.clip(jax.random.uniform(own_keys[2], (ANGLES,), jnp.float32, -0.4, 0.4) * block_scale(own_keys[2], (ANGLES,), ((0, 2),), -0.4, 0.0), -0.4, 0.4),
    }


courant = 0.9
coupling = 0.2


def slopes(fields, cosine, sine_phase, detuning):
    inner_cells = fields[:, :, 1:-1]
    behind = fields[:, :, :-2]
    ahead_cells = fields[:, :, 2:]
    trans_real = -courant * (inner_cells[0] - behind[0]) - coupling * (sine_phase * inner_cells[2] + cosine * inner_cells[3])
    trans_imag = -courant * (inner_cells[1] - behind[1]) + coupling * (cosine * inner_cells[2] - sine_phase * inner_cells[3])
    bragg_real = courant * (ahead_cells[2] - inner_cells[2]) - coupling * (cosine * inner_cells[1] - sine_phase * inner_cells[0]) - detuning * inner_cells[3]
    bragg_imag = courant * (ahead_cells[3] - inner_cells[3]) + coupling * (cosine * inner_cells[0] + sine_phase * inner_cells[1]) + detuning * inner_cells[2]
    return jnp.stack([trans_real, trans_imag, bragg_real, bragg_imag])


def heun_plane(fields, cosine, sine_phase, detuning):
    padding = ((0, 0), (0, 0), (1, 1), (0, 0))
    slope_one = slopes(jnp.pad(fields, padding), cosine, sine_phase, detuning)
    trial_step = fields + slope_one
    slope_two = slopes(jnp.pad(trial_step, padding), cosine, sine_phase, detuning)
    return fields + 0.5 * (slope_one + slope_two)


def reference(incident, phase, deviation):
    angles = deviation.shape[0]
    entrance = jnp.broadcast_to(incident[:, None], (2, angles) + incident.shape[1:])
    fields = jnp.concatenate([entrance, jnp.zeros_like(entrance)], axis=0)
    detuning = deviation[:, None, None]
    collected = []
    for depth_plane in range(NZ):
        cosine = jnp.cos(phase[depth_plane])
        sine_phase = jnp.sin(phase[depth_plane])
        fields = heun_plane(fields, cosine, sine_phase, detuning)
        if (depth_plane + 1) % PLANES == 0:
            collected.append(fields)
    return jnp.stack(collected)
```

```python
import functools
import math

import jax
import jax.numpy as jnp
import numpy as np
from jax import lax
from jax.experimental import pallas as pl
from jax.experimental.pallas import tpu as pltpu
from jax.sharding import PartitionSpec as P

courant = np.float32(0.9)
coupling = np.float32(0.2)


nu = float(courant)
stay = float(np.float32(1.0) - courant) / nu
amplitude = float(coupling) / nu
carry = 1.0 / nu**2


def half_angle_series():
    z = np.linspace(0.0, math.pi**2 * 1.0001, 20001)
    y = np.sqrt(z) / 2
    sine = np.where(y > 0, np.sin(y) / np.maximum(2 * y, 1e-30), 0.5)
    cheb, power = np.polynomial.Chebyshev, np.polynomial.Polynomial
    fits = [cheb.fit(z, v, d).convert(kind=power).coef for v, d in ((sine, 5), (np.cos(y), 6))]
    return [[float(c) for c in fit] for fit in fits]


sine_series, cosine_series = half_angle_series()


def horner(series, z):
    total = series[-1] * z + series[-2]
    for c in series[-3::-1]:
        total = total * z + c
    return total


def scaled_sincos(phi, scale):
    z = phi * phi
    s = horner(sine_series, z) * phi
    t = s * (2.0 * scale)
    return t * horner(cosine_series, z), scale - t * s


def pick(index, values):
    out = values[-1]
    for i in range(len(values) - 2, -1, -1):
        out = jnp.where(index == i, values[i], out)
    return out


def columns_at(ref, index, count, block):
    if block % 128 == 0:
        return ref[:, :, pl.ds(pl.multiple_of(index * block, block), block)]
    return pick(index, [ref[:, :, i * block : (i + 1) * block] for i in range(count)])


def pack_kernel(meta, phase, incident, *outs, sections):
    planes, rows, block = outs[0].shape
    width = 2 * planes
    own, entrance, sends = outs[0], outs[1], outs[2:]
    depth, odd = meta[0], meta[1]
    entrance[...] = columns_at(incident, meta[4] * sections + depth, incident.shape[2] // block, block)
    for shift in range(sections):
        target = lax.rem(depth + shift, sections)
        if shift == 0:
            full, even_pairs, odd_pairs = own, sends[0], sends[1]
        else:
            full, even_pairs, odd_pairs = sends[3 * shift - 1 : 3 * shift + 2]
        full[...] = columns_at(phase, target, sections, block)

        def fill(up_ref, down_ref):
            base = rows - width
            for p in range(planes // 2):
                q = planes - 1 - p
                n = 2 * p + 1
                up_ref[p] = full[p, base:rows, :]
                up_ref[p, 0:n, :] = full[q, rows - n : rows, :]
                down_ref[p] = full[p, 0:width, :]
                down_ref[p, width - n : width, :] = full[q, 0:n, :]
            if shift == 0:
                for c in range(2):
                    up_ref[planes // 2 + c] = entrance[c, base:rows, :]
                    down_ref[planes // 2 + c] = entrance[c, 0:width, :]

        @pl.when(odd == 0)
        def _():
            fill(even_pairs, odd_pairs)

        @pl.when(odd == 1)
        def _():
            fill(odd_pairs, even_pairs)


def slab_kernel(meta, detuning, *refs, sections, slab, planes, rows):
    width = 2 * planes
    odd, lower, upper = meta[1], meta[2] > 0, meta[3] > 0
    source = lax.rem(meta[0] - slab + sections, sections)
    phases, refs = refs[: 3 * sections], refs[3 * sections :]
    starts, refs = refs[:3], refs[3:]
    out, v0, v1, w, cs, ss = refs
    angles = out.shape[0]

    def side(refs_even, refs_odd, *at):
        even, odds = pick(source, [r[at] for r in refs_even]), pick(source, [r[at] for r in refs_odd])
        return jnp.where(odd == 0, odds, even), jnp.where(odd == 0, even, odds)

    full, even_pairs, odd_pairs = phases[0::3], phases[1::3], phases[2::3]
    low_scale = jnp.where(lower, amplitude, 0.0)
    high_scale = jnp.where(upper, amplitude, 0.0)
    for p in range(planes // 2):
        q = planes - 1 - p
        below, above = side(even_pairs, odd_pairs, p)
        for at, n, block, scale in (
            (0, width - 1 - 2 * p, below, low_scale),
            (width + rows, 2 * p + 1 - width, above, high_scale),
        ):
            for table, value in zip((ss, cs), scaled_sincos(block, scale)):
                table[p, at : at + width, :] = value
                table[q, at + n : at + n + width, :] = value
    for p in range(planes):
        block = pick(source, [r[p] for r in full])
        ss[p, width : width + rows, :], cs[p, width : width + rows, :] = scaled_sincos(block, amplitude)

    blank = jnp.zeros((width, out.shape[3]), jnp.float32)
    for a in range(angles):
        for c in range(4):
            if slab == 0:
                own, even_halo, odd_halo = starts
                if c < 2:
                    even, odds = even_halo[planes // 2 + c], odd_halo[planes // 2 + c]
                    middle = own[c]
                else:
                    even = odds = blank
                    middle = jnp.zeros((rows, out.shape[3]), jnp.float32)
                below, above = jnp.where(odd == 0, odds, even), jnp.where(odd == 0, even, odds)
            else:
                own, even_halo, odd_halo = starts
                middle = own[a, c]
                below = jnp.where(odd == 0, odd_halo[a, c, rows - width :, :], even_halo[a, c, rows - width :, :])
                above = jnp.where(odd == 0, even_halo[a, c, :width, :], odd_halo[a, c, :width, :])
            v0[a, c, 0:width, :] = jnp.where(lower, below, 0.0)
            v0[a, c, width : width + rows, :] = middle
            v0[a, c, width + rows : 2 * width + rows, :] = jnp.where(upper, above, 0.0)

    def euler(ref, a, at, sine, cosine, turn):
        here = slice(at, at + 8)
        tr, ti, br, bi = (ref[a, c, here, :] for c in range(4))
        tr_back, ti_back = (ref[a, c, at - 1 : at + 7, :] for c in (0, 1))
        br_next, bi_next = (ref[a, c, at + 1 : at + 9, :] for c in (2, 3))
        return (
            (stay * tr + tr_back) - (sine * br + cosine * bi),
            (stay * ti + ti_back) + (cosine * br - sine * bi),
            (stay * br + br_next) - (cosine * ti - sine * tr) - turn * bi,
            (stay * bi + bi_next) + (cosine * tr + sine * ti) + turn * br,
        )

    turns = [detuning[a] * (1.0 / nu) for a in range(angles)]
    now, later = v0, v1
    for p in range(planes):
        reach = 2 * (planes - p) - 1
        for at in range(width - reach, width + rows + reach, 8):
            sine, cosine = ss[p, at : at + 8, :], cs[p, at : at + 8, :]
            for a in range(angles):
                for c, value in enumerate(euler(now, a, at, sine, cosine, turns[a])):
                    w[a, c, at : at + 8, :] = value
        reach -= 1
        for at in range(width - reach, width + rows + reach, 8):
            sine, cosine = ss[p, at : at + 8, :], cs[p, at : at + 8, :]
            for a in range(angles):
                for c, value in enumerate(euler(w, a, at, sine, cosine, turns[a])):
                    later[a, c, at : at + 8, :] = carry * now[a, c, at : at + 8, :] + value
        now, later = later, now
    shrink = (nu**2 / 2.0) ** planes
    for a in range(angles):
        for c in range(4):
            out[a, c] = shrink * now[a, c, width : width + rows, :]


VMEM = pl.BlockSpec(memory_space=pltpu.VMEM)
SMEM = pl.BlockSpec(memory_space=pltpu.SMEM)


def neighbours(lat, sections, cores, parity, shift):
    pairs = []
    for row in range(lat):
        other = row + 1 if row % 2 == parity else row - 1
        for depth in range(sections):
            for core in range(cores):
                here = (row * sections + depth) * cores + core
                if 0 <= other < lat:
                    there = (other * sections + (depth + shift) % sections) * cores + core
                else:
                    there = (row * sections + depth) * cores + (core + 1) % cores
                pairs.append((here, there))
    return pairs


def on_device(incident, phase, deviation):
    planes, rows, columns = phase.shape
    lat, sections, cores = (lax.axis_size(a) for a in ("lat", "depth", "rock"))
    row, depth, core = (lax.axis_index(a) for a in ("lat", "depth", "rock"))
    angles = cores * deviation.shape[0]
    block = columns // sections
    width = 2 * planes
    assert rows >= width and planes % 2 == 0
    everyone = ("lat", "depth", "rock")

    def from_neighbour(value, parity, shift):
        return lax.ppermute(value, everyone, neighbours(lat, sections, cores, parity, shift))

    def route(value, shift, turn):
        pairs = []
        for d in range(sections):
            for c in range(cores):
                pairs.append((d * cores + c, (d + shift) % sections * cores + (c + turn) % cores))
        return lax.ppermute(value, ("depth", "rock"), pairs)

    meta = jnp.stack([depth, row % 2, row > 0, row + 1 < lat, core]).astype(jnp.int32)
    shape = lambda *dims: jax.ShapeDtypeStruct(dims, jnp.float32)
    outs = [shape(planes, rows, block), shape(2, rows, block)]
    outs += [shape(planes // 2 + 2, width, block)] * 2
    for _ in range(1, sections):
        outs += [shape(planes, rows, block)] + [shape(planes // 2, width, block)] * 2
    packed = pl.pallas_call(
        functools.partial(pack_kernel, sections=sections),
        out_shape=outs,
        in_specs=[SMEM, VMEM, VMEM],
        out_specs=[VMEM] * len(outs),
        name="pack",
    )(meta, phase, incident)
    own, entrance, sends = packed[0], packed[1], packed[2:]
    detuning = [deviation]
    for turn in range(1, cores):
        detuning.append(route(deviation, 0, turn))
    detuning = jnp.concatenate(detuning)
    received = [own, from_neighbour(sends[0], 0, 0), from_neighbour(sends[1], 1, 0)]
    for shift in range(1, sections):
        full, even, odd = sends[3 * shift - 1 : 3 * shift + 2]
        received += [route(full, shift, 0), from_neighbour(even, 0, shift), from_neighbour(odd, 1, shift)]

    starts = [entrance, received[1], received[2]]
    exits = []
    window = rows + 2 * width + 16
    for slab in range(sections):
        fields = pl.pallas_call(
            functools.partial(slab_kernel, sections=sections, slab=slab, planes=planes, rows=rows),
            out_shape=shape(angles, 4, rows, block),
            in_specs=[SMEM, SMEM] + [VMEM] * (len(received) + 3),
            out_specs=VMEM,
            scratch_shapes=[pltpu.VMEM((angles, 4, window, block), jnp.float32)] * 3
            + [pltpu.VMEM((planes, window, block), jnp.float32)] * 2,
            name=f"slab{slab}",
        )(meta, detuning, *received, *starts)
        exits.append(fields)
        if slab + 1 < sections:
            starts = [fields, from_neighbour(fields, 0, 0), from_neighbour(fields, 1, 0)]

    pieces = {}
    for shift in range(sections):
        mine = pick(lax.rem(depth + shift, sections), exits)
        for turn in range(cores):
            piece = mine[turn]
            pieces[shift, turn] = piece if shift == 0 and turn == 0 else route(piece, shift, turn)
    tiles = []
    for c in range(cores):
        for d in range(sections):
            by_turn = []
            for turn in range(cores):
                by_turn.append(pick(lax.rem(depth - d + sections, sections), [pieces[s, turn] for s in range(sections)]))
            tiles.append(pick(lax.rem(core - c + cores, cores), by_turn))
    return jnp.concatenate(tiles, axis=2)[None, :, None]


def solution(mesh):
    placed = (
        P(None, ("groups", "lat"), None),
        P("depth", ("groups", "lat"), "rock"),
        P(("groups", "rock")),
    )
    return jax.shard_map(
        on_device,
        mesh=mesh,
        in_specs=placed,
        out_specs=P("depth", None, "rock", ("groups", "lat"), None),
        check_vma=False,
    )
```

```python
import functools
import math

import jax
import jax.numpy as jnp
import numpy as np
from jax import lax
from jax.experimental import pallas as pl
from jax.experimental.pallas import tpu as pltpu
from jax.sharding import PartitionSpec as P

courant = np.float32(0.9)
coupling = np.float32(0.2)


nu = float(courant)
stay = float(np.float32(1.0) - courant) / nu
amplitude = float(coupling) / nu
carry = 1.0 / nu**2


def half_angle_series():
    z = np.linspace(0.0, math.pi**2 * 1.0001, 20001)
    y = np.sqrt(z) / 2
    sine = np.where(y > 0, np.sin(y) / np.maximum(2 * y, 1e-30), 0.5)
    cheb, power = np.polynomial.Chebyshev, np.polynomial.Polynomial
    fits = [cheb.fit(z, v, d).convert(kind=power).coef for v, d in ((sine, 5), (np.cos(y), 6))]
    return [[float(c) for c in fit] for fit in fits]


sine_series, cosine_series = half_angle_series()


def horner(series, z):
    total = series[-1] * z + series[-2]
    for c in series[-3::-1]:
        total = total * z + c
    return total


def scaled_sincos(phi, scale):
    z = phi * phi
    s = horner(sine_series, z) * phi
    t = s * (2.0 * scale)
    return t * horner(cosine_series, z), scale - t * s


def pick(index, values):
    out = values[-1]
    for i in range(len(values) - 2, -1, -1):
        out = jnp.where(index == i, values[i], out)
    return out


def columns_at(ref, index, count, block):
    if block % 128 == 0:
        return ref[:, :, pl.ds(pl.multiple_of(index * block, block), block)]
    return pick(index, [ref[:, :, i * block : (i + 1) * block] for i in range(count)])


def position():
    row = lax.axis_index("lat")
    return lax.axis_index("depth"), lax.rem(row, 2), row > 0, row + 1 < lax.axis_size("lat")


def pack_kernel(detuning, phase, incident, *outs, sections):
    planes, rows, block = outs[0].shape
    width = 2 * planes
    own, entrance, turns, sends = outs[0], outs[1], outs[2], outs[3:]
    depth, odd, _, _ = position()
    for a in range(turns.shape[0]):
        turns[a] = jnp.full(turns.shape[1:], detuning[a] * (1.0 / nu))
    which = lax.axis_index("rock") * sections + depth
    entrance[...] = columns_at(incident, which, incident.shape[2] // block, block)
    for shift in range(sections):
        target = lax.rem(depth + shift, sections)
        if shift == 0:
            full, even_pairs, odd_pairs = own, sends[0], sends[1]
        else:
            full, even_pairs, odd_pairs = sends[3 * shift - 1 : 3 * shift + 2]
        full[...] = columns_at(phase, target, sections, block)

        def fill(up_ref, down_ref):
            base = rows - width
            for p in range(planes // 2):
                q = planes - 1 - p
                n = 2 * p + 1
                up_ref[p] = full[p, base:rows, :]
                up_ref[p, 0:n, :] = full[q, rows - n : rows, :]
                down_ref[p] = full[p, 0:width, :]
                down_ref[p, width - n : width, :] = full[q, 0:n, :]
            if shift == 0:
                for c in range(2):
                    up_ref[planes // 2 + c] = entrance[c, base:rows, :]
                    down_ref[planes // 2 + c] = entrance[c, 0:width, :]

        @pl.when(odd == 0)
        def _():
            fill(even_pairs, odd_pairs)

        @pl.when(odd == 1)
        def _():
            fill(odd_pairs, even_pairs)


def slab_kernel(*refs, sections, slab, cores, planes, rows):
    width = 2 * planes
    depth, odd, lower, upper = position()
    source = lax.rem(depth - slab + sections, sections)
    turn_refs, refs = refs[:cores], refs[cores:]
    phases, refs = refs[: 3 * sections], refs[3 * sections :]
    starts, refs = refs[:3], refs[3:]
    out, v0, v1, w, cs, ss = refs
    angles = out.shape[0]

    def side(refs_even, refs_odd, *at):
        even, odds = pick(source, [r[at] for r in refs_even]), pick(source, [r[at] for r in refs_odd])
        return jnp.where(odd == 0, odds, even), jnp.where(odd == 0, even, odds)

    full, even_pairs, odd_pairs = phases[0::3], phases[1::3], phases[2::3]
    low_scale = jnp.where(lower, amplitude, 0.0)
    high_scale = jnp.where(upper, amplitude, 0.0)
    for p in range(planes // 2):
        q = planes - 1 - p
        below, above = side(even_pairs, odd_pairs, p)
        for at, n, block, scale in (
            (0, width - 1 - 2 * p, below, low_scale),
            (width + rows, 2 * p + 1 - width, above, high_scale),
        ):
            for table, value in zip((ss, cs), scaled_sincos(block, scale)):
                table[p, at : at + width, :] = value
                table[q, at + n : at + n + width, :] = value
    for p in range(planes):
        block = pick(source, [r[p] for r in full])
        ss[p, width : width + rows, :], cs[p, width : width + rows, :] = scaled_sincos(block, amplitude)

    blank = jnp.zeros((width, out.shape[3]), jnp.float32)
    for a in range(angles):
        for c in range(4):
            if slab == 0:
                own, even_halo, odd_halo = starts
                if c < 2:
                    even, odds = even_halo[planes // 2 + c], odd_halo[planes // 2 + c]
                    middle = own[c]
                else:
                    even = odds = blank
                    middle = jnp.zeros((rows, out.shape[3]), jnp.float32)
                below, above = jnp.where(odd == 0, odds, even), jnp.where(odd == 0, even, odds)
            else:
                own, even_halo, odd_halo = starts
                middle = own[a, c]
                below = jnp.where(odd == 0, odd_halo[a, c, rows - width :, :], even_halo[a, c, rows - width :, :])
                above = jnp.where(odd == 0, even_halo[a, c, :width, :], odd_halo[a, c, :width, :])
            v0[a, c, 0:width, :] = jnp.where(lower, below, 0.0)
            v0[a, c, width : width + rows, :] = middle
            v0[a, c, width + rows : 2 * width + rows, :] = jnp.where(upper, above, 0.0)

    def euler(ref, a, at, sine, cosine, turn):
        here = slice(at, at + 8)
        tr, ti, br, bi = (ref[a, c, here, :] for c in range(4))
        tr_back, ti_back = (ref[a, c, at - 1 : at + 7, :] for c in (0, 1))
        br_next, bi_next = (ref[a, c, at + 1 : at + 9, :] for c in (2, 3))
        return (
            (stay * tr + tr_back) - (sine * br + cosine * bi),
            (stay * ti + ti_back) + (cosine * br - sine * bi),
            (stay * br + br_next) - (cosine * ti - sine * tr) - turn * bi,
            (stay * bi + bi_next) + (cosine * tr + sine * ti) + turn * br,
        )

    turns = [ref[a] for ref in turn_refs for a in range(ref.shape[0])]
    now, later = v0, v1
    for p in range(planes):
        reach = 2 * (planes - p) - 1
        for at in range(width - reach, width + rows + reach, 8):
            sine, cosine = ss[p, at : at + 8, :], cs[p, at : at + 8, :]
            for a in range(angles):
                for c, value in enumerate(euler(now, a, at, sine, cosine, turns[a])):
                    w[a, c, at : at + 8, :] = value
        reach -= 1
        for at in range(width - reach, width + rows + reach, 8):
            sine, cosine = ss[p, at : at + 8, :], cs[p, at : at + 8, :]
            for a in range(angles):
                for c, value in enumerate(euler(w, a, at, sine, cosine, turns[a])):
                    later[a, c, at : at + 8, :] = carry * now[a, c, at : at + 8, :] + value
        now, later = later, now
    shrink = (nu**2 / 2.0) ** planes
    for a in range(angles):
        for c in range(4):
            out[a, c] = shrink * now[a, c, width : width + rows, :]


VMEM = pl.BlockSpec(memory_space=pltpu.VMEM)
SMEM = pl.BlockSpec(memory_space=pltpu.SMEM)
GRANT = pltpu.CompilerParams(vmem_limit_bytes=16 * 2**20)


def neighbours(lat, sections, cores, parity, shift):
    pairs = []
    for row in range(lat):
        other = row + 1 if row % 2 == parity else row - 1
        for depth in range(sections):
            for core in range(cores):
                here = (row * sections + depth) * cores + core
                if 0 <= other < lat:
                    there = (other * sections + (depth + shift) % sections) * cores + core
                else:
                    there = (row * sections + depth) * cores + (core + 1) % cores
                pairs.append((here, there))
    return pairs


def on_device(incident, phase, deviation):
    planes, rows, columns = phase.shape
    lat, sections, cores = (lax.axis_size(a) for a in ("lat", "depth", "rock"))
    row, depth, core = (lax.axis_index(a) for a in ("lat", "depth", "rock"))
    angles = cores * deviation.shape[0]
    block = columns // sections
    width = 2 * planes
    assert rows >= width and planes % 2 == 0
    everyone = ("lat", "depth", "rock")

    def from_neighbour(value, parity, shift):
        return lax.ppermute(value, everyone, neighbours(lat, sections, cores, parity, shift))

    def route(value, shift, turn):
        pairs = []
        for d in range(sections):
            for c in range(cores):
                pairs.append((d * cores + c, (d + shift) % sections * cores + (c + turn) % cores))
        return lax.ppermute(value, ("depth", "rock"), pairs)

    shape = lambda *dims: jax.ShapeDtypeStruct(dims, jnp.float32)
    outs = [shape(planes, rows, block), shape(2, rows, block), shape(deviation.shape[0], 8, block)]
    outs += [shape(planes // 2 + 2, width, block)] * 2
    for _ in range(1, sections):
        outs += [shape(planes, rows, block)] + [shape(planes // 2, width, block)] * 2
    packed = pl.pallas_call(
        functools.partial(pack_kernel, sections=sections),
        out_shape=outs,
        in_specs=[SMEM, VMEM, VMEM],
        out_specs=[VMEM] * len(outs),
        compiler_params=GRANT,
        name="pack",
    )(deviation, phase, incident)
    own, entrance, turns, sends = packed[0], packed[1], packed[2], packed[3:]
    turns = [turns] + [route(turns, 0, turn) for turn in range(1, cores)]
    received = [own, from_neighbour(sends[0], 0, 0), from_neighbour(sends[1], 1, 0)]
    for shift in range(1, sections):
        full, even, odd = sends[3 * shift - 1 : 3 * shift + 2]
        received += [route(full, shift, 0), from_neighbour(even, 0, shift), from_neighbour(odd, 1, shift)]

    starts = [entrance, received[1], received[2]]
    exits = []
    window = rows + 2 * width + 16
    for slab in range(sections):
        fields = pl.pallas_call(
            functools.partial(slab_kernel, sections=sections, slab=slab, cores=cores, planes=planes, rows=rows),
            out_shape=shape(angles, 4, rows, block),
            in_specs=[VMEM] * (cores + len(received) + 3),
            out_specs=VMEM,
            scratch_shapes=[pltpu.VMEM((angles, 4, window, block), jnp.float32)] * 3
            + [pltpu.VMEM((planes, window, block), jnp.float32)] * 2,
            compiler_params=GRANT,
            name=f"slab{slab}",
        )(*turns, *received, *starts)
        exits.append(fields)
        if slab + 1 < sections:
            starts = [fields, from_neighbour(fields, 0, 0), from_neighbour(fields, 1, 0)]

    pieces = {}
    for shift in range(sections):
        mine = pick(lax.rem(depth + shift, sections), exits)
        for turn in range(cores):
            piece = mine[turn]
            pieces[shift, turn] = piece if shift == 0 and turn == 0 else route(piece, shift, turn)
    tiles = []
    for c in range(cores):
        for d in range(sections):
            by_turn = []
            for turn in range(cores):
                by_turn.append(pick(lax.rem(depth - d + sections, sections), [pieces[s, turn] for s in range(sections)]))
            tiles.append(pick(lax.rem(core - c + cores, cores), by_turn))
    return jnp.concatenate(tiles, axis=2)[None, :, None]


def solution(mesh):
    placed = (
        P(None, ("groups", "lat"), None),
        P("depth", ("groups", "lat"), "rock"),
        P(("groups", "rock")),
    )
    return jax.shard_map(
        on_device,
        mesh=mesh,
        in_specs=placed,
        out_specs=P("depth", None, "rock", ("groups", "lat"), None),
        check_vma=False,
    )
```

```python
import functools
import math

import jax
import jax.numpy as jnp
import numpy as np
from jax import lax
from jax.experimental import pallas as pl
from jax.experimental.pallas import tpu as pltpu
from jax.sharding import PartitionSpec as P

courant = np.float32(0.9)
coupling = np.float32(0.2)


nu = float(courant)
stay = float(np.float32(1.0) - courant) / nu
amplitude = float(coupling) / nu
carry = 1.0 / nu**2


def half_angle_series():
    z = np.linspace(0.0, math.pi**2 * 1.0001, 20001)
    y = np.sqrt(z) / 2
    sine = np.where(y > 0, np.sin(y) / np.maximum(2 * y, 1e-30), 0.5)
    cheb, power = np.polynomial.Chebyshev, np.polynomial.Polynomial
    fits = [cheb.fit(z, v, d).convert(kind=power).coef for v, d in ((sine, 5), (np.cos(y), 6))]
    return [[float(c) for c in fit] for fit in fits]


sine_series, cosine_series = half_angle_series()


def horner(series, z):
    total = series[-1] * z + series[-2]
    for c in series[-3::-1]:
        total = total * z + c
    return total


def scaled_sincos(phi, scale):
    z = phi * phi
    s = horner(sine_series, z) * phi
    t = s * (2.0 * scale)
    return t * horner(cosine_series, z), scale - t * s


def pick(index, values):
    out = values[-1]
    for i in range(len(values) - 2, -1, -1):
        out = jnp.where(index == i, values[i], out)
    return out


def columns_at(ref, index, count, block):
    if block % 128 == 0:
        return ref[:, :, pl.ds(pl.multiple_of(index * block, block), block)]
    return pick(index, [ref[:, :, i * block : (i + 1) * block] for i in range(count)])


def halo_kind(planes, rows, sections, slab, distance):
    need = [2 * ((sections - slab) * planes - p) - 1 - (distance - 1) * rows for p in range(planes)]
    if need[0] <= 0:
        return None
    return "triangle" if planes % 2 == 0 and need[0] == rows - 1 and rows == 2 * planes else "full"


def swaps(lat, sections, cores, distance, parity):
    pairs, real = [], False
    for row in range(lat):
        other = row + distance if row // distance % 2 == parity else row - distance
        real |= 0 <= other < lat
        for depth in range(sections):
            for core in range(cores):
                here = (row * sections + depth) * cores + core
                if 0 <= other < lat:
                    there = (other * sections + depth) * cores + core
                else:
                    there = (row * sections + depth) * cores + (core + 1) % cores
                pairs.append((here, there))
    return pairs if real else None


def columns_kernel(detuning, phase, incident, *outs, sections):
    block = outs[0].shape[2]
    entrance, turns, parts = outs[0], outs[1], outs[2:]
    depth = lax.axis_index("depth")
    for a in range(turns.shape[0]):
        turns[a] = jnp.full(turns.shape[1:], detuning[a] * (1.0 / nu))
    which = lax.axis_index("rock") * sections + depth
    entrance[...] = columns_at(incident, which, incident.shape[2] // block, block)
    for shift in range(sections):
        parts[shift][...] = columns_at(phase, lax.rem(depth + shift, sections), sections, block)


def pack_kernel(entrance, *refs, sections, wanted):
    parts, sends = refs[:sections], refs[sections:]
    planes, rows, block = parts[0].shape
    depth, row = lax.axis_index("depth"), lax.axis_index("lat")

    def fill(distance, up, down):
        at = 0
        for slab in range(sections):
            kind = halo_kind(planes, rows, sections, slab, distance)
            source = lax.rem(depth - slab + sections, sections)
            take = lambda p: pick(source, [r[p] for r in parts])
            if kind == "full":
                for p in range(planes):
                    value = take(p)
                    for ref in (up, down):
                        if ref is not None:
                            ref[at + p] = value
                at += planes
            elif kind == "triangle":
                for p in range(planes // 2):
                    n = 2 * p + 1
                    value, other = take(p), take(planes - 1 - p)
                    if up is not None:
                        up[at + p] = value
                        up[at + p, 0:n, :] = other[rows - n :]
                    if down is not None:
                        down[at + p] = value
                        down[at + p, rows - n :, :] = other[:n]
                at += planes // 2
        for c in range(2):
            for ref in (up, down):
                if ref is not None:
                    ref[at + c] = entrance[c]

    for distance in sorted({d for d, _ in wanted}):
        pair = [sends[wanted.index((distance, q))] if (distance, q) in wanted else None for q in (0, 1)]
        for q in (0, 1):
            pl.when(lax.rem(row // distance, 2) == q)(functools.partial(fill, distance, pair[q], pair[1 - q]))


def march_kernel(*refs, sections, cores, wanted, reach):
    turn_refs, entrance, refs = refs[:cores], refs[cores], refs[cores + 1 :]
    parts, halos, refs = refs[:sections], refs[sections : sections + len(wanted)], refs[sections + len(wanted) :]
    outs, (v0, v1, w, cs, ss) = refs[:-5], refs[-5:]
    planes, rows, block = parts[0].shape
    angles = v0.shape[0]
    total = planes * sections
    width = reach * rows
    depth, row, lat = lax.axis_index("depth"), lax.axis_index("lat"), lax.axis_size("lat")

    blank = jnp.zeros((rows, block), jnp.float32)

    def sides(distance, at):
        even, odd = (halos[wanted.index((distance, q))][at] if (distance, q) in wanted else None for q in (0, 1))
        if even is None and odd is None:
            return blank, blank
        if even is None or odd is None:
            value = odd if even is None else even
            return value, value
        first = lax.rem(row // distance, 2) == 0
        return jnp.where(first, odd, even), jnp.where(first, even, odd)

    for distance in range(reach, 0, -1):
        lower, upper = row >= distance, row + distance < lat
        scales = [jnp.where(inside, amplitude, 0.0) for inside in (lower, upper)]
        places = (width - distance * rows, width + distance * rows)
        at = 0
        for slab in range(sections):
            kind = halo_kind(planes, rows, sections, slab, distance)
            first = slab * planes
            for p in range({None: 0, "full": planes, "triangle": planes // 2}[kind]):
                n = rows - 1 - 2 * p
                for place, scale, value, skew in zip(places, scales, sides(distance, at + p), (n, -n)):
                    for ref, entry in zip((ss, cs), scaled_sincos(value, scale)):
                        ref[first + p, place : place + rows, :] = entry
                        if kind == "triangle":
                            ref[first + planes - 1 - p, place + skew : place + skew + rows, :] = entry
            at += {None: 0, "full": planes, "triangle": planes // 2}[kind]
        for c in range(4):
            values = sides(distance, at + c) if c < 2 else (blank, blank)
            for place, inside, value in zip(places, (lower, upper), values):
                for a in range(angles):
                    v0[a, c, place : place + rows, :] = jnp.where(inside, value, 0.0)
    for c in range(4):
        for a in range(angles):
            v0[a, c, width : width + rows, :] = entrance[c] if c < 2 else blank
    for slab in range(sections):
        source = lax.rem(depth - slab + sections, sections)
        for p in range(planes):
            value = pick(source, [r[p] for r in parts])
            for ref, entry in zip((ss, cs), scaled_sincos(value, amplitude)):
                ref[slab * planes + p, width : width + rows, :] = entry

    def euler(ref, a, at, sine, cosine, turn):
        here = slice(at, at + 8)
        tr, ti, br, bi = (ref[a, c, here, :] for c in range(4))
        tr_back, ti_back = (ref[a, c, at - 1 : at + 7, :] for c in (0, 1))
        br_next, bi_next = (ref[a, c, at + 1 : at + 9, :] for c in (2, 3))
        return (
            (stay * tr + tr_back) - (sine * br + cosine * bi),
            (stay * ti + ti_back) + (cosine * br - sine * bi),
            (stay * br + br_next) - (cosine * ti - sine * tr) - turn * bi,
            (stay * bi + bi_next) + (cosine * tr + sine * ti) + turn * br,
        )

    turns = [ref[a] for ref in turn_refs for a in range(ref.shape[0])]
    now, later = v0, v1
    for p in range(total):
        span = 2 * (total - p) - 1
        for at in range(width - span, width + rows + span, 8):
            sine, cosine = ss[p, at : at + 8, :], cs[p, at : at + 8, :]
            for a in range(angles):
                for c, value in enumerate(euler(now, a, at, sine, cosine, turns[a])):
                    w[a, c, at : at + 8, :] = value
        span = 2 * (total - p) - 2
        for at in range(width - span, width + rows + span, 8):
            sine, cosine = ss[p, at : at + 8, :], cs[p, at : at + 8, :]
            for a in range(angles):
                for c, value in enumerate(euler(w, a, at, sine, cosine, turns[a])):
                    later[a, c, at : at + 8, :] = carry * now[a, c, at : at + 8, :] + value
        now, later = later, now
        if (p + 1) % planes == 0:
            shrink = (nu**2 / 2.0) ** (p + 1)
            shift = lax.rem(p // planes - depth + sections, sections)

            def leave(s, now=now, shrink=shrink):
                for a in range(angles):
                    for c in range(4):
                        outs[s * angles + a][c] = shrink * now[a, c, width : width + rows, :]

            for s in range(sections):
                pl.when(shift == s)(functools.partial(leave, s))


VMEM = pl.BlockSpec(memory_space=pltpu.VMEM)
SMEM = pl.BlockSpec(memory_space=pltpu.SMEM)
GRANT = pltpu.CompilerParams(vmem_limit_bytes=24 * 2**20)


def kernel_call(kernel, name, shapes, in_specs, scratch=()):
    return pl.pallas_call(
        kernel,
        out_shape=[jax.ShapeDtypeStruct(s, jnp.float32) for s in shapes],
        in_specs=in_specs,
        out_specs=[VMEM] * len(shapes),
        scratch_shapes=[pltpu.VMEM(s, jnp.float32) for s in scratch],
        compiler_params=GRANT,
        name=name,
    )


def on_device(incident, phase, deviation):
    planes, rows, columns = phase.shape
    lat, sections, cores = (lax.axis_size(a) for a in ("lat", "depth", "rock"))
    depth, core = lax.axis_index("depth"), lax.axis_index("rock")
    angles = cores * deviation.shape[0]
    block = columns // sections
    reach = -(-2 * planes * sections // rows)

    def route(value, shift, turn):
        pairs = []
        for d in range(sections):
            for c in range(cores):
                pairs.append((d * cores + c, (d + shift) % sections * cores + (c + turn) % cores))
        return lax.ppermute(value, ("depth", "rock"), pairs)

    shapes = [(2, rows, block), (deviation.shape[0], 8, block)] + [(planes, rows, block)] * sections
    split = functools.partial(columns_kernel, sections=sections)
    entrance, turns, *parts = kernel_call(split, "columns", shapes, [SMEM, VMEM, VMEM])(deviation, phase, incident)
    parts = [parts[0]] + [route(parts[s], s, 0) for s in range(1, sections)]
    turns = [turns] + [route(turns, 0, turn) for turn in range(1, cores)]

    wanted, pairs, shapes = [], [], []
    for distance in range(1, reach + 1):
        kinds = [halo_kind(planes, rows, sections, slab, distance) for slab in range(sections)]
        depths = sum({None: 0, "full": planes, "triangle": planes // 2}[kind] for kind in kinds)
        for parity in (0, 1):
            swap = swaps(lat, sections, cores, distance, parity)
            if swap is not None:
                wanted.append((distance, parity))
                pairs.append(swap)
                shapes.append((depths + 2, rows, block))
    pack = functools.partial(pack_kernel, sections=sections, wanted=wanted)
    sends = kernel_call(pack, "pack", shapes, [VMEM] * (1 + sections))(entrance, *parts)
    halos = [lax.ppermute(s, ("lat", "depth", "rock"), swap) for s, swap in zip(sends, pairs)]

    window = rows * (2 * reach + 1) + 16
    march = functools.partial(march_kernel, sections=sections, cores=cores, wanted=wanted, reach=reach)
    exits = kernel_call(
        march,
        "march",
        [(4, rows, block)] * (sections * angles),
        [VMEM] * (cores + 1 + sections + len(halos)),
        [(angles, 4, window, block)] * 3 + [(sections * planes, window, block)] * 2,
    )(*turns, entrance, *parts, *halos)

    pieces = {}
    for shift in range(sections):
        for turn in range(cores):
            piece = exits[shift * angles + turn]
            pieces[shift, turn] = piece if shift == 0 and turn == 0 else route(piece, shift, turn)
    tiles = []
    for c in range(cores):
        for d in range(sections):
            by_turn = []
            for turn in range(cores):
                by_turn.append(pick(lax.rem(depth - d + sections, sections), [pieces[s, turn] for s in range(sections)]))
            tiles.append(pick(lax.rem(core - c + cores, cores), by_turn))
    return jnp.concatenate(tiles, axis=2)[None, :, None]


def solution(mesh):
    placed = (
        P(None, ("groups", "lat"), None),
        P("depth", ("groups", "lat"), "rock"),
        P(("groups", "rock")),
    )
    return jax.shard_map(
        on_device,
        mesh=mesh,
        in_specs=placed,
        out_specs=P("depth", None, "rock", ("groups", "lat"), None),
        check_vma=False,
    )
```

```python
import functools
import math

import jax
import jax.numpy as jnp
import numpy as np
from jax import lax
from jax.experimental import pallas as pl
from jax.experimental.pallas import tpu as pltpu
from jax.sharding import PartitionSpec as P


courant = np.float32(0.9)
coupling = np.float32(0.2)


nu = float(courant)
stay = float(np.float32(1.0) - courant) / nu
amplitude = float(coupling) / nu
carry = 1.0 / nu**2


def half_angle_series():
    z = np.linspace(0.0, math.pi**2 * 1.0001, 20001)
    y = np.sqrt(z) / 2
    sine = np.where(y > 0, np.sin(y) / np.maximum(2 * y, 1e-30), 0.5)
    cheb, power = np.polynomial.Chebyshev, np.polynomial.Polynomial
    fits = [cheb.fit(z, v, d).convert(kind=power).coef for v, d in ((sine, 5), (np.cos(y), 6))]
    return [[float(c) for c in fit] for fit in fits]


sine_series, cosine_series = half_angle_series()


def horner(series, z):
    total = series[-1] * z + series[-2]
    for c in series[-3::-1]:
        total = total * z + c
    return total


def scaled_sincos(phi, scale):
    z = phi * phi
    s = horner(sine_series, z) * phi
    t = s * (2.0 * scale)
    return t * horner(cosine_series, z), scale - t * s


def pick(index, values):
    out = values[-1]
    for i in range(len(values) - 2, -1, -1):
        out = jnp.where(index == i, values[i], out)
    return out


def columns_at(ref, index, count, block):
    if block % 128 == 0:
        return ref[:, :, pl.ds(pl.multiple_of(index * block, block), block)]
    return pick(index, [ref[:, :, i * block : (i + 1) * block] for i in range(count)])


def halo_kind(planes, rows, sections, slab, distance):
    need = [2 * ((sections - slab) * planes - p) - 1 - (distance - 1) * rows for p in range(planes)]
    if need[0] <= 0:
        return None
    return "triangle" if planes % 2 == 0 and need[0] == rows - 1 and rows == 2 * planes else "full"


def swaps(lat, sections, cores, distance, parity, shift, useful):
    pairs, real = [], False
    for row in range(lat):
        other = row + distance if row // distance % 2 == parity else row - distance
        real |= 0 <= other < lat
        for depth in range(sections):
            for core in range(cores):
                target, aim, to = row, (depth + shift) % sections, core
                if 0 <= other < lat and depth in useful:
                    target = other
                elif shift == 0 or not 0 <= other < lat:
                    aim, to = depth, (core + 1) % cores
                pairs.append(((row * sections + depth) * cores + core, (target * sections + aim) * cores + to))
    assert len({b for _, b in pairs}) == len(pairs)
    return pairs if real else None


def pieces_of(kind, planes):
    return {None: 0, "full": planes, "triangle": planes // 2}[kind]


def write_halo(kind, planes, rows, take, up, down, at):
    for p in range(pieces_of(kind, planes)):
        value = take(p)
        for ref in (up, down):
            if ref is not None:
                ref[at + p] = value
        if kind == "triangle":
            n, other = 2 * p + 1, take(planes - 1 - p)
            if up is not None:
                up[at + p, 0:n, :] = other[rows - n :]
            if down is not None:
                down[at + p, rows - n :, :] = other[:n]


def columns_kernel(detuning, phase_hbm, incident_hbm, *refs, sections, far):
    outs, (phase, incident, sems) = refs[:-3], refs[-3:]
    planes, rows, columns = phase.shape
    block = columns // sections
    entrance, turns, parts, sends = outs[0], outs[1], outs[2 : 2 + sections], outs[2 + sections :]
    depth, row = lax.axis_index("depth"), lax.axis_index("lat")
    mine = pl.ds(pl.multiple_of(lax.axis_index("rock") * columns, columns), columns)
    loads = [
        pltpu.make_async_copy(phase_hbm, phase, sems.at[0]),
        pltpu.make_async_copy(incident_hbm.at[:, :, mine], incident, sems.at[1]),
    ]
    for load in loads:
        load.start()
    for a in range(turns.shape[0]):
        turns[a] = jnp.full(turns.shape[1:], detuning[a] * (1.0 / nu))
    for load in loads:
        load.wait()
    entrance[...] = columns_at(incident, depth, sections, block)
    for shift in range(sections):
        parts[shift][...] = columns_at(phase, lax.rem(depth + shift, sections), sections, block)

    def fill(shift, kind, up, down):
        at = up.shape[0] - 2 if up is not None else down.shape[0] - 2
        write_halo(kind, planes, rows, lambda p: parts[shift][p], up, down, 0)
        fields = columns_at(incident, lax.rem(depth + shift, sections), sections, block)
        for ref in (up, down):
            if ref is not None:
                ref[at : at + 2] = fields

    for distance, shift in sorted({(d, s) for d, _, s in far}):
        pair = [sends[far.index((distance, q, shift))] if (distance, q, shift) in far else None for q in (0, 1)]
        for slab in range(sections):
            kind = halo_kind(planes, rows, sections, slab, distance)
            if kind is None and slab > 0:
                continue
            for q in (0, 1):
                here = (depth == slab) & (lax.rem(row // distance, 2) == q)
                pl.when(here)(functools.partial(fill, shift, kind, pair[q], pair[1 - q]))


def hand_on(source, target):
    target[...] = source[...]


def pack_kernel(entrance, *refs, sections):
    parts, sends = refs[:sections], refs[sections:]
    planes, rows, _ = parts[0].shape
    depth, row = lax.axis_index("depth"), lax.axis_index("lat")

    def fill(up, down):
        at = 0
        for slab in range(sections):
            kind = halo_kind(planes, rows, sections, slab, 1)
            source = lax.rem(depth - slab + sections, sections)
            write_halo(kind, planes, rows, lambda p: pick(source, [r[p] for r in parts]), up, down, at)
            at += pieces_of(kind, planes)
        for ref in (up, down):
            if ref is not None:
                ref[at : at + 2] = entrance[...]

    pair = [sends[q] if q < len(sends) else None for q in (0, 1)]
    for q in (0, 1):
        pl.when(lax.rem(row, 2) == q)(functools.partial(fill, pair[q], pair[1 - q]))


def march_kernel(*refs, sections, cores, near, far, reach):
    turn_refs, entrance, refs = refs[:cores], refs[cores], refs[cores + 1 :]
    parts, refs = refs[:sections], refs[sections:]
    halos, refs = dict(zip(near + far, refs)), refs[len(near + far) :]
    outs, (v0, v1, w, cs, ss) = refs[:-5], refs[-5:]
    planes, rows, block = parts[0].shape
    angles = v0.shape[0]
    total = planes * sections
    width = reach * rows
    depth, row, lat = lax.axis_index("depth"), lax.axis_index("lat"), lax.axis_size("lat")

    blank = jnp.zeros((rows, block), jnp.float32)

    def sides(distance, source, at):
        even, odd = (
            pick(source, [halos[distance, q, s][at] for s in range(sections if distance > 1 else 1)])
            if (distance, q, 0) in halos
            else blank
            for q in (0, 1)
        )
        first = lax.rem(row // distance, 2) == 0
        return jnp.where(first, odd, even), jnp.where(first, even, odd)

    for distance in range(reach, 0, -1):
        lower, upper = row >= distance, row + distance < lat
        scales = [jnp.where(inside, amplitude, 0.0) for inside in (lower, upper)]
        places = (width - distance * rows, width + distance * rows)
        at = 0
        for slab in range(sections):
            kind = halo_kind(planes, rows, sections, slab, distance)
            first = slab * planes
            source = lax.rem(depth - slab + sections, sections)
            at = at if distance == 1 else 0
            for p in range(pieces_of(kind, planes)):
                n = rows - 1 - 2 * p
                for place, scale, value, skew in zip(places, scales, sides(distance, source, at + p), (n, -n)):
                    for ref, entry in zip((ss, cs), scaled_sincos(value, scale)):
                        ref[first + p, place : place + rows, :] = entry
                        if kind == "triangle":
                            ref[first + planes - 1 - p, place + skew : place + skew + rows, :] = entry
            at += pieces_of(kind, planes)
        if distance > 1:
            at = max(pieces_of(halo_kind(planes, rows, sections, slab, distance), planes) for slab in range(sections))
        for c in range(4):
            values = sides(distance, depth, at + c) if c < 2 else (blank, blank)
            for place, inside, value in zip(places, (lower, upper), values):
                for a in range(angles):
                    v0[a, c, place : place + rows, :] = jnp.where(inside, value, 0.0)
    for c in range(4):
        for a in range(angles):
            v0[a, c, width : width + rows, :] = entrance[c] if c < 2 else blank
    for slab in range(sections):
        source = lax.rem(depth - slab + sections, sections)
        for p in range(planes):
            value = pick(source, [r[p] for r in parts])
            for ref, entry in zip((ss, cs), scaled_sincos(value, amplitude)):
                ref[slab * planes + p, width : width + rows, :] = entry

    def euler(ref, a, at, sine, cosine, turn):
        here = slice(at, at + 8)
        tr, ti, br, bi = (ref[a, c, here, :] for c in range(4))
        tr_back, ti_back = (ref[a, c, at - 1 : at + 7, :] for c in (0, 1))
        br_next, bi_next = (ref[a, c, at + 1 : at + 9, :] for c in (2, 3))
        return (
            (stay * tr + tr_back) - (sine * br + cosine * bi),
            (stay * ti + ti_back) + (cosine * br - sine * bi),
            (stay * br + br_next) - (cosine * ti - sine * tr) - turn * bi,
            (stay * bi + bi_next) + (cosine * tr + sine * ti) + turn * br,
        )

    turns = [ref[a] for ref in turn_refs for a in range(ref.shape[0])]
    now, later = v0, v1
    for p in range(total):
        span = 2 * (total - p) - 1
        for at in range(width - span, width + rows + span, 8):
            sine, cosine = ss[p, at : at + 8, :], cs[p, at : at + 8, :]
            for a in range(angles):
                for c, value in enumerate(euler(now, a, at, sine, cosine, turns[a])):
                    w[a, c, at : at + 8, :] = value
        span = 2 * (total - p) - 2
        for at in range(width - span, width + rows + span, 8):
            sine, cosine = ss[p, at : at + 8, :], cs[p, at : at + 8, :]
            for a in range(angles):
                for c, value in enumerate(euler(w, a, at, sine, cosine, turns[a])):
                    later[a, c, at : at + 8, :] = carry * now[a, c, at : at + 8, :] + value
        now, later = later, now
        if (p + 1) % planes == 0:
            shrink = (nu**2 / 2.0) ** (p + 1)
            shift = lax.rem(p // planes - depth + sections, sections)

            def leave(s, now=now, shrink=shrink):
                for a in range(angles):
                    for c in range(4):
                        outs[s * angles + a][c] = shrink * now[a, c, width : width + rows, :]

            for s in range(sections):
                pl.when(shift == s)(functools.partial(leave, s))


VMEM = pl.BlockSpec(memory_space=pltpu.VMEM)
SMEM = pl.BlockSpec(memory_space=pltpu.SMEM)
HBM = pl.BlockSpec(memory_space=pltpu.HBM)
GRANT = pltpu.CompilerParams(vmem_limit_bytes=24 * 2**20)


def kernel_call(kernel, shapes, in_specs, scratch=()):
    return pl.pallas_call(
        kernel,
        out_shape=[jax.ShapeDtypeStruct(s, jnp.float32) for s in shapes],
        in_specs=in_specs,
        out_specs=[VMEM] * len(shapes),
        scratch_shapes=[pltpu.VMEM(s, jnp.float32) if isinstance(s, tuple) else s for s in scratch],
        compiler_params=GRANT,
    )


def scattered(incident, phase, deviation):
    planes, rows, columns = phase.shape
    lat, sections, cores = (lax.axis_size(a) for a in ("lat", "depth", "rock"))
    depth, core = lax.axis_index("depth"), lax.axis_index("rock")
    angles = cores * deviation.shape[0]
    block = columns // sections
    reach = -(-2 * planes * sections // rows)

    def route(value, shift, turn):
        pairs = []
        for d in range(sections):
            for c in range(cores):
                pairs.append((d * cores + c, (d + shift) % sections * cores + (c + turn) % cores))
        return lax.ppermute(value, ("depth", "rock"), pairs)

    near, far, routes, shapes = [], [], {}, []
    for distance in range(1, reach + 1):
        kinds = [halo_kind(planes, rows, sections, slab, distance) for slab in range(sections)]
        useful = [slab for slab in range(sections) if slab == 0 or distance == 1 or kinds[slab]]
        for shift in range(sections if distance > 1 else 1):
            for parity in (0, 1):
                swap = swaps(lat, sections, cores, distance, parity, shift, useful)
                if swap is not None:
                    (far if distance > 1 else near).append((distance, parity, shift))
                    routes[distance, parity, shift] = swap
                    if distance > 1:
                        shapes.append((max(pieces_of(kind, planes) for kind in kinds) + 2, rows, block))
    shapes = [(2, rows, block), (deviation.shape[0], 8, block)] + [(planes, rows, block)] * sections + shapes
    split = functools.partial(columns_kernel, sections=sections, far=far)
    scratch = [(planes, rows, columns), (2, rows, columns), pltpu.SemaphoreType.DMA((2,))]
    stored = (pltpu.with_memory_space_constraint(a, pltpu.HBM) for a in (phase, incident))
    entrance, turns, *parts = kernel_call(split, shapes, [SMEM, HBM, HBM], scratch)(deviation, *stored)
    parts, sends = parts[:sections], parts[sections:]
    everyone = ("lat", "depth", "rock")
    parts = [parts[0]] + [route(parts[s], s, 0) for s in range(1, sections)]
    turns = [turns] + [route(turns, 0, turn) for turn in range(1, cores)]
    far_halos = [lax.ppermute(s, everyone, routes[key]) for s, key in zip(sends, far)]
    (entrance,) = kernel_call(hand_on, [(2, rows, block)], [VMEM])(entrance)
    depths = sum(pieces_of(halo_kind(planes, rows, sections, slab, 1), planes) for slab in range(sections))
    pack = functools.partial(pack_kernel, sections=sections)
    sends = kernel_call(pack, [(depths + 2, rows, block)] * len(near), [VMEM] * (1 + sections))(entrance, *parts)
    halos = [lax.ppermute(s, everyone, routes[key]) for s, key in zip(sends, near)] + far_halos

    window = rows * (2 * reach + 1) + 16
    march = functools.partial(march_kernel, sections=sections, cores=cores, near=near, far=far, reach=reach)
    exits = kernel_call(
        march,
        [(4, rows, block)] * (sections * angles),
        [VMEM] * (cores + 1 + sections + len(halos)),
        [(angles, 4, window, block)] * 3 + [(sections * planes, window, block)] * 2,
    )(*turns, entrance, *parts, *halos)

    pieces = {}
    for shift in range(sections):
        for turn in range(cores):
            piece = exits[shift * angles + turn]
            pieces[shift, turn] = piece if shift == 0 and turn == 0 else route(piece, shift, turn)
    tiles = []
    for c in range(cores):
        for d in range(sections):
            by_turn = []
            for turn in range(cores):
                by_turn.append(pick(lax.rem(depth - d + sections, sections), [pieces[s, turn] for s in range(sections)]))
            tiles.append(pick(lax.rem(core - c + cores, cores), by_turn))
    return jnp.concatenate(tiles, axis=2)[None, :, None]


def solution(mesh):
    placed = (
        P(None, ("groups", "lat"), None),
        P("depth", ("groups", "lat"), "rock"),
        P(("groups", "rock")),
    )
    return jax.shard_map(
        scattered,
        mesh=mesh,
        in_specs=placed,
        out_specs=P("depth", None, "rock", ("groups", "lat"), None),
        check_vma=False,
    )
```

```python
import functools
import math

import jax
import jax.numpy as jnp
import numpy as np
from jax import lax
from jax.experimental import pallas as pl
from jax.experimental.pallas import tpu as pltpu
from jax.sharding import PartitionSpec as P


courant = np.float32(0.9)
coupling = np.float32(0.2)


nu = float(courant)
stay = float(np.float32(1.0) - courant) / nu
amplitude = float(coupling) / nu
carry = 1.0 / nu**2


def half_angle_series():
    z = np.linspace(0.0, math.pi**2 * 1.0001, 20001)
    y = np.sqrt(z) / 2
    sine = np.where(y > 0, np.sin(y) / np.maximum(2 * y, 1e-30), 0.5)
    cheb, power = np.polynomial.Chebyshev, np.polynomial.Polynomial
    fits = [cheb.fit(z, v, d).convert(kind=power).coef for v, d in ((sine, 5), (np.cos(y), 6))]
    return [[float(c) for c in fit] for fit in fits]


sine_series, cosine_series = half_angle_series()


def horner(series, z):
    total = series[-1] * z + series[-2]
    for c in series[-3::-1]:
        total = total * z + c
    return total


def scaled_sincos(phi, scale):
    z = phi * phi
    s = horner(sine_series, z) * phi
    t = s * (2.0 * scale)
    return t * horner(cosine_series, z), scale - t * s


def pick(index, values):
    out = values[-1]
    for i in range(len(values) - 2, -1, -1):
        out = jnp.where(index == i, values[i], out)
    return out


def columns_at(ref, index, count, block):
    if block % 128 == 0:
        return ref[:, :, pl.ds(pl.multiple_of(index * block, block), block)]
    return pick(index, [ref[:, :, i * block : (i + 1) * block] for i in range(count)])


def halo_kind(planes, rows, sections, slab, distance):
    need = [2 * ((sections - slab) * planes - p) - 1 - (distance - 1) * rows for p in range(planes)]
    if need[0] <= 0:
        return None
    return "triangle" if planes % 2 == 0 and need[0] == rows - 1 and rows == 2 * planes else "full"


def swaps(lat, sections, cores, distance, parity, shift, useful):
    pairs, real = [], False
    for row in range(lat):
        other = row + distance if row // distance % 2 == parity else row - distance
        real |= 0 <= other < lat
        for depth in range(sections):
            for core in range(cores):
                target, aim, to = row, (depth + shift) % sections, core
                if 0 <= other < lat and depth in useful:
                    target = other
                elif shift == 0 or not 0 <= other < lat:
                    aim, to = depth, (core + 1) % cores
                pairs.append(((row * sections + depth) * cores + core, (target * sections + aim) * cores + to))
    assert len({b for _, b in pairs}) == len(pairs)
    return pairs if real else None


def pieces_of(kind, planes):
    return {None: 0, "full": planes, "triangle": planes // 2}[kind]


def write_halo(kind, planes, rows, take, up, down, at):
    for p in range(pieces_of(kind, planes)):
        value = take(p)
        for ref in (up, down):
            if ref is not None:
                ref[at + p] = value
        if kind == "triangle":
            n, other = 2 * p + 1, take(planes - 1 - p)
            if up is not None:
                up[at + p, 0:n, :] = other[rows - n :]
            if down is not None:
                down[at + p, rows - n :, :] = other[:n]


def columns_kernel(detuning, phase_hbm, incident_hbm, *refs, sections, far):
    outs, (phase, incident, sems) = refs[:-3], refs[-3:]
    planes, rows, columns = phase.shape
    block = columns // sections
    entrance, turns, parts, sends = outs[0], outs[1], outs[2 : 2 + sections], outs[2 + sections :]
    depth, row = lax.axis_index("depth"), lax.axis_index("lat")
    mine = pl.ds(pl.multiple_of(lax.axis_index("rock") * columns, columns), columns)
    loads = [
        pltpu.make_async_copy(phase_hbm, phase, sems.at[0]),
        pltpu.make_async_copy(incident_hbm.at[:, :, mine], incident, sems.at[1]),
    ]
    for load in loads:
        load.start()
    for a in range(turns.shape[0]):
        turns[a] = jnp.full(turns.shape[1:], detuning[a] * (1.0 / nu))
    for load in loads:
        load.wait()
    entrance[...] = columns_at(incident, depth, sections, block)
    for shift in range(sections):
        parts[shift][...] = columns_at(phase, lax.rem(depth + shift, sections), sections, block)

    def fill(shift, kind, up, down):
        at = up.shape[0] - 2 if up is not None else down.shape[0] - 2
        write_halo(kind, planes, rows, lambda p: parts[shift][p], up, down, 0)
        fields = columns_at(incident, lax.rem(depth + shift, sections), sections, block)
        for ref in (up, down):
            if ref is not None:
                ref[at : at + 2] = fields

    for distance, shift in sorted({(d, s) for d, _, s in far}):
        pair = [sends[far.index((distance, q, shift))] if (distance, q, shift) in far else None for q in (0, 1)]
        for slab in range(sections):
            kind = halo_kind(planes, rows, sections, slab, distance)
            if kind is None and slab > 0:
                continue
            for q in (0, 1):
                here = (depth == slab) & (lax.rem(row // distance, 2) == q)
                pl.when(here)(functools.partial(fill, shift, kind, pair[q], pair[1 - q]))


def hand_on(source, target):
    target[...] = source[...]


def pack_kernel(entrance, *refs, sections):
    parts, sends = refs[:sections], refs[sections:]
    planes, rows, _ = parts[0].shape
    depth, row = lax.axis_index("depth"), lax.axis_index("lat")

    def fill(up, down):
        at = 0
        for slab in range(sections):
            kind = halo_kind(planes, rows, sections, slab, 1)
            source = lax.rem(depth - slab + sections, sections)
            write_halo(kind, planes, rows, lambda p: pick(source, [r[p] for r in parts]), up, down, at)
            at += pieces_of(kind, planes)
        for ref in (up, down):
            if ref is not None:
                ref[at : at + 2] = entrance[...]

    pair = [sends[q] if q < len(sends) else None for q in (0, 1)]
    for q in (0, 1):
        pl.when(lax.rem(row, 2) == q)(functools.partial(fill, pair[q], pair[1 - q]))


def march_kernel(*refs, sections, cores, near, far, reach):
    turn_refs, entrance, refs = refs[:cores], refs[cores], refs[cores + 1 :]
    parts, refs = refs[:sections], refs[sections:]
    halos, refs = dict(zip(near + far, refs)), refs[len(near + far) :]
    outs, (v0, v1, w, cs, ss) = refs[:-5], refs[-5:]
    planes, rows, block = parts[0].shape
    angles = v0.shape[0]
    total = planes * sections
    width = reach * rows
    depth, row, lat = lax.axis_index("depth"), lax.axis_index("lat"), lax.axis_size("lat")

    blank = jnp.zeros((rows, block), jnp.float32)

    def sides(distance, source, at):
        even, odd = (
            pick(source, [halos[distance, q, s][at] for s in range(sections if distance > 1 else 1)])
            if (distance, q, 0) in halos
            else blank
            for q in (0, 1)
        )
        first = lax.rem(row // distance, 2) == 0
        return jnp.where(first, odd, even), jnp.where(first, even, odd)

    for distance in range(reach, 0, -1):
        lower, upper = row >= distance, row + distance < lat
        scales = [jnp.where(inside, amplitude, 0.0) for inside in (lower, upper)]
        places = (width - distance * rows, width + distance * rows)
        at = 0
        for slab in range(sections):
            kind = halo_kind(planes, rows, sections, slab, distance)
            first = slab * planes
            source = lax.rem(depth - slab + sections, sections)
            at = at if distance == 1 else 0
            for p in range(pieces_of(kind, planes)):
                n = rows - 1 - 2 * p
                blocks = sides(distance, source, at + p)
                for place, inside, scale, value, skew in zip(places, (lower, upper), scales, blocks, (n, -n)):
                    value = jnp.where(inside, value, 0.0)
                    for ref, entry in zip((ss, cs), scaled_sincos(value, scale)):
                        ref[first + p, place : place + rows, :] = entry
                        if kind == "triangle":
                            ref[first + planes - 1 - p, place + skew : place + skew + rows, :] = entry
            at += pieces_of(kind, planes)
        if distance > 1:
            at = max(pieces_of(halo_kind(planes, rows, sections, slab, distance), planes) for slab in range(sections))
        for c in range(4):
            values = sides(distance, depth, at + c) if c < 2 else (blank, blank)
            for place, inside, value in zip(places, (lower, upper), values):
                for a in range(angles):
                    v0[a, c, place : place + rows, :] = jnp.where(inside, value, 0.0)
    for c in range(4):
        for a in range(angles):
            v0[a, c, width : width + rows, :] = entrance[c] if c < 2 else blank
    for slab in range(sections):
        source = lax.rem(depth - slab + sections, sections)
        for p in range(planes):
            value = pick(source, [r[p] for r in parts])
            for ref, entry in zip((ss, cs), scaled_sincos(value, amplitude)):
                ref[slab * planes + p, width : width + rows, :] = entry

    def euler(ref, a, at, sine, cosine, turn):
        here = slice(at, at + 8)
        tr, ti, br, bi = (ref[a, c, here, :] for c in range(4))
        tr_back, ti_back = (ref[a, c, at - 1 : at + 7, :] for c in (0, 1))
        br_next, bi_next = (ref[a, c, at + 1 : at + 9, :] for c in (2, 3))
        return (
            (stay * tr + tr_back) - (sine * br + cosine * bi),
            (stay * ti + ti_back) + (cosine * br - sine * bi),
            (stay * br + br_next) - (cosine * ti - sine * tr) - turn * bi,
            (stay * bi + bi_next) + (cosine * tr + sine * ti) + turn * br,
        )

    turns = [ref[a] for ref in turn_refs for a in range(ref.shape[0])]
    now, later = v0, v1
    for p in range(total):
        span = 2 * (total - p) - 1
        for at in range(width - span, width + rows + span, 8):
            sine, cosine = ss[p, at : at + 8, :], cs[p, at : at + 8, :]
            for a in range(angles):
                for c, value in enumerate(euler(now, a, at, sine, cosine, turns[a])):
                    w[a, c, at : at + 8, :] = value
        span = 2 * (total - p) - 2
        for at in range(width - span, width + rows + span, 8):
            sine, cosine = ss[p, at : at + 8, :], cs[p, at : at + 8, :]
            for a in range(angles):
                for c, value in enumerate(euler(w, a, at, sine, cosine, turns[a])):
                    later[a, c, at : at + 8, :] = carry * now[a, c, at : at + 8, :] + value
        now, later = later, now
        if (p + 1) % planes == 0:
            shrink = (nu**2 / 2.0) ** (p + 1)
            shift = lax.rem(p // planes - depth + sections, sections)

            def leave(s, now=now, shrink=shrink):
                for a in range(angles):
                    for c in range(4):
                        outs[s * angles + a][c] = shrink * now[a, c, width : width + rows, :]

            for s in range(sections):
                pl.when(shift == s)(functools.partial(leave, s))


VMEM = pl.BlockSpec(memory_space=pltpu.VMEM)
SMEM = pl.BlockSpec(memory_space=pltpu.SMEM)
HBM = pl.BlockSpec(memory_space=pltpu.HBM)
GRANT = pltpu.CompilerParams(vmem_limit_bytes=24 * 2**20)


def kernel_call(kernel, shapes, in_specs, scratch=()):
    return pl.pallas_call(
        kernel,
        out_shape=[jax.ShapeDtypeStruct(s, jnp.float32) for s in shapes],
        in_specs=in_specs,
        out_specs=[VMEM] * len(shapes),
        scratch_shapes=[pltpu.VMEM(s, jnp.float32) if isinstance(s, tuple) else s for s in scratch],
        compiler_params=GRANT,
    )


def scattered(incident, phase, deviation):
    planes, rows, columns = phase.shape
    lat, sections, cores = (lax.axis_size(a) for a in ("lat", "depth", "rock"))
    depth, core = lax.axis_index("depth"), lax.axis_index("rock")
    angles = cores * deviation.shape[0]
    block = columns // sections
    reach = -(-2 * planes * sections // rows)

    def route(value, shift, turn):
        pairs = []
        for d in range(sections):
            for c in range(cores):
                pairs.append((d * cores + c, (d + shift) % sections * cores + (c + turn) % cores))
        return lax.ppermute(value, ("depth", "rock"), pairs)

    near, far, routes, shapes = [], [], {}, []
    for distance in range(1, reach + 1):
        kinds = [halo_kind(planes, rows, sections, slab, distance) for slab in range(sections)]
        useful = [slab for slab in range(sections) if slab == 0 or distance == 1 or kinds[slab]]
        for shift in range(sections if distance > 1 else 1):
            for parity in (0, 1):
                swap = swaps(lat, sections, cores, distance, parity, shift, useful)
                if swap is not None:
                    (far if distance > 1 else near).append((distance, parity, shift))
                    routes[distance, parity, shift] = swap
                    if distance > 1:
                        shapes.append((max(pieces_of(kind, planes) for kind in kinds) + 2, rows, block))
    shapes = [(2, rows, block), (deviation.shape[0], 8, block)] + [(planes, rows, block)] * sections + shapes
    split = functools.partial(columns_kernel, sections=sections, far=far)
    scratch = [(planes, rows, columns), (2, rows, columns), pltpu.SemaphoreType.DMA((2,))]
    stored = (pltpu.with_memory_space_constraint(a, pltpu.HBM) for a in (phase, incident))
    entrance, turns, *parts = kernel_call(split, shapes, [SMEM, HBM, HBM], scratch)(deviation, *stored)
    parts, sends = parts[:sections], parts[sections:]
    everyone = ("lat", "depth", "rock")
    parts = [parts[0]] + [route(parts[s], s, 0) for s in range(1, sections)]
    turns = [turns] + [route(turns, 0, turn) for turn in range(1, cores)]
    far_halos = []
    for key, send in zip(far, sends):
        far_halos.append(lax.ppermute(send, everyone, routes[key]))
    (entrance,) = kernel_call(hand_on, [(2, rows, block)], [VMEM])(entrance)
    depths = sum(pieces_of(halo_kind(planes, rows, sections, slab, 1), planes) for slab in range(sections))
    pack = functools.partial(pack_kernel, sections=sections)
    sends = kernel_call(pack, [(depths + 2, rows, block)] * len(near), [VMEM] * (1 + sections))(entrance, *parts)
    halos = []
    for key, send in zip(near, sends):
        halos.append(lax.ppermute(send, everyone, routes[key]))
    halos += far_halos

    window = rows * (2 * reach + 1) + 16
    march = functools.partial(march_kernel, sections=sections, cores=cores, near=near, far=far, reach=reach)
    exits = kernel_call(
        march,
        [(4, rows, block)] * (sections * angles),
        [VMEM] * (cores + 1 + sections + len(halos)),
        [(angles, 4, window, block)] * 3 + [(sections * planes, window, block)] * 2,
    )(*turns, entrance, *parts, *halos)

    pieces = {}
    for shift in range(sections):
        for turn in range(cores):
            piece = exits[shift * angles + turn]
            pieces[shift, turn] = piece if shift == 0 and turn == 0 else route(piece, shift, turn)
    tiles = []
    for c in range(cores):
        for d in range(sections):
            by_turn = []
            for turn in range(cores):
                by_turn.append(pick(lax.rem(depth - d + sections, sections), [pieces[s, turn] for s in range(sections)]))
            tiles.append(pick(lax.rem(core - c + cores, cores), by_turn))
    return jnp.concatenate(tiles, axis=2)[None, :, None]


def solution(mesh):
    placed = (
        P(None, ("groups", "lat"), None),
        P("depth", ("groups", "lat"), "rock"),
        P(("groups", "rock")),
    )
    return jax.shard_map(
        scattered,
        mesh=mesh,
        in_specs=placed,
        out_specs=P("depth", None, "rock", ("groups", "lat"), None),
        check_vma=False,
    )
```
